128 devices in a mesh: blk: 64 (over y, x_lo, z, core), tile: 2 (over x_hi).
Axes of the slice: x: 4 (x_hi: 2, x_lo: 2; x = x_hi * 2 + x_lo), y: 4, z: 4, core: 2. Of those that a mesh axis runs over, the one named last changes fastest.
Arguments:
- positions: float32 [3, 8192], P(None, ('blk', 'tile')), as said below
- noise_vectors: float32 [3, 32, 8192], P(None, None, ('blk', 'tile')), may hold values from -6 to 6
- spectrum_bounds: float32 [2], replicated, as said below
Outputs:
- displacement: float32 [3, 32, 8192], P(None, None, ('blk', 'tile'))
- images: float32 [2, 3, 32, 8192], P(None, None, None, ('blk', 'tile'))
The draws below stay inside these ranges and needn't reach their ends.
Inputs may be any that keep to these rules, and one draw needn't show every extreme that they name: `positions`: coordinates lie in a cube whose edge is the cube root of 41.9 * 8192; particle n's third coordinate lies between n and n + 1 times that edge divided by 8192. `spectrum_bounds`: the first entry lies between 0.15 and 0.35; the second exceeds 50 times the first.
All inputs are finite; a program needn't handle non-finite values.
Results may differ from the reference program's by a relative error of at most 0.0003.
Values sent between devices are 32-bit elements; how exact they have to be, the bound alone decides.
A program may use at most 64 MiB of HBM per device.

```python
import math
import jax
import jax.numpy as jnp
from jax import lax

PART_DEV = 64
NOISE = 32
NPART = 8192


def cube_edge():
    return (41.9 * NPART) ** (1.0 / 3.0)


def draw_positions(key, part):
    edge_value = cube_edge()
    split_keys = jax.random.split(key, 2)
    lateral = jax.random.uniform(split_keys[0], (2, NPART), jnp.float32)
    height_axis = (jnp.arange(NPART, dtype=jnp.float32) + jax.random.uniform(split_keys[1], (NPART,), jnp.float32)) * (edge_value / NPART)
    return jnp.concatenate([lateral * edge_value, height_axis[None, :]], axis=0)


def draw_noise_vectors(key, part):
    split_keys = jax.random.split(jax.random.fold_in(key, 17), 1)
    return jax.random.truncated_normal(split_keys[0], -6.0, 6.0, (3, NOISE, NPART), jnp.float32)


def draw_spectrum_bounds(key, part):
    estimate = 2.5 * NPART / cube_edge()
    sample = jax.random.uniform(key, (2,), jnp.float32)
    return jnp.stack([0.15 + 0.2 * sample[0], estimate * (0.9 + 0.4 * sample[1])])


def setup_inputs(seed: int = 0) -> dict:
    splits = jax.random.split(jax.random.key(seed), 4)
    positions = draw_positions(jax.random.fold_in(splits[3], 71), 0)
    noise_vectors = draw_noise_vectors(jax.random.fold_in(splits[3], 71), 0)
    spectrum_bounds = draw_spectrum_bounds(jax.random.fold_in(splits[3], 71), 0)
    return dict(positions=positions, noise_vectors=noise_vectors, spectrum_bounds=spectrum_bounds)


soft_core = 1e-06
node_count = 32

def kernel(targets, sources):
    offset = targets[:, :, None] - sources[:, None, :]
    squared = lax.optimization_barrier(jnp.sum(offset * offset, axis=0)) + soft_core
    distance = jnp.sqrt(squared)
    inverse = 1.0 / distance
    cubed = inverse * inverse * inverse
    intersection = distance < 2.0
    scalar_part = jnp.where(intersection, 1.0 - 0.28125 * distance, 0.75 * inverse + 0.5 * cubed)
    dyadic_part = jnp.where(intersection, 0.09375 * inverse, 0.75 * cubed - 1.5 * cubed * inverse * inverse)
    identity = jnp.eye(3, dtype=targets.dtype)
    return identity[:, :, None, None] * scalar_part[None, None] + dyadic_part[None, None] * offset[:, None] * offset[None, :]

def contract(tensor, vectors):
    return jnp.einsum('abij,bkj->aki', tensor, vectors, precision=lax.Precision.HIGHEST)

def weights_from(bounds):
    lowest = bounds[0]
    highest = bounds[1]
    center = 0.5 * (highest + lowest)
    spread = 0.5 * (highest - lowest)
    angles = math.pi * (jnp.arange(node_count, dtype=bounds.dtype) + 0.5) / node_count
    samples = jnp.sqrt(center + spread * jnp.cos(angles))
    weights = [2.0 / node_count * jnp.sum(samples * jnp.cos(order * angles)) for order in range(3)]
    return (center, spread, weights)

def mobility(vectors, positions):
    groups = NPART // PART_DEV
    targets = positions.reshape(3, groups, PART_DEV).transpose(1, 0, 2)

    def one_group(target_rows):
        return contract(kernel(target_rows, positions), vectors)
    pieces = lax.map(one_group, targets)
    return pieces.transpose(1, 2, 0, 3).reshape(3, vectors.shape[1], NPART)

def reference(positions, noise_vectors, spectrum_bounds):
    center, spread, weights = weights_from(spectrum_bounds)
    first_image = mobility(noise_vectors, positions)
    linear_term = (first_image - center * noise_vectors) / spread
    second_image = mobility(linear_term, positions)
    quadratic_term = 2.0 * (second_image - center * linear_term) / spread - noise_vectors
    displacement = 0.5 * weights[0] * noise_vectors + weights[1] * linear_term + weights[2] * quadratic_term
    return (displacement, jnp.stack([first_image, second_image]))
```

```python
import math

import jax
import jax.numpy as jnp
from jax import lax
from jax.experimental import pallas as pl
from jax.experimental.pallas import tpu as pltpu
from jax.sharding import PartitionSpec as P

MESH = pl.DeviceIdType.MESH
F32 = jnp.float32
BF16 = jnp.bfloat16

soft_core = 1e-06
node_count = 32
edge = (41.9 * 8192) ** (1.0 / 3.0)
middle = 0.5 * edge

own = 64
packed = 48
n_src = 8
n_tgt = 16
J = n_src * own

SOURCES = [(0, 0), (1, 0), (3, 0), (0, 1), (2, 0), (1, 1), (3, 1), (2, 1)]


def coords():
    block = lax.axis_index("blk")
    half = lax.axis_index("tile")
    return block // 16, (block // 8) % 2, (block // 2) % 4, block % 2, half


def source_peer(slot):
    dy, flip = SOURCES[slot]
    y, low, z, core, high = coords()
    return ((((y + dy) % 4) * 2 + (low + flip) % 2) * 4 + z) * 2 + core, high


def target_peer(slot):
    quarter = slot // 4
    dz = (2 + 3 * quarter + (quarter // 2) * (3 + 2 * (quarter % 2))) % 4
    flip = 1 - (slot // 2) % 2
    swap = 1 - slot % 2
    y, low, z, core, high = coords()
    return (
        ((y * 2 + (low + flip) % 2) * 4 + (z + dz) % 4) * 2 + (core + swap) % 2,
        (high + flip) % 2,
    )


def remote(src, dst, send, recv, device):
    return pltpu.make_async_remote_copy(
        src_ref=src, dst_ref=dst, send_sem=send, recv_sem=recv, device_id=device, device_id_type=MESH
    )


def lanes(rows):
    return lax.broadcasted_iota(jnp.int32, (rows, 128), 1)


def pack(full):
    tail = full[packed:own]
    moved = jnp.concatenate([pltpu.roll(tail, 96 - 32 * g, 1) if g < 3 else tail for g in range(3)], axis=0)
    return jnp.where(lanes(packed) < 96, full[:packed], moved)


def unpack(block):
    l16 = lanes(16)
    parts = [pltpu.roll(block[16 * g : 16 * g + 16], 32 + 32 * g, 1) for g in range(3)]
    tail = jnp.where(l16 < 32, parts[0], jnp.where(l16 < 64, parts[1], parts[2]))
    return jnp.concatenate([block, tail], axis=0)


def split(value):
    high = value.astype(BF16)
    low = (value - high.astype(F32)).astype(BF16)
    return high, low


def body_kernel(
    pos_ref, noise_ref, bounds_ref, disp_ref, img_ref,
    square, ptile, tpos, spos, srow, scol, tcol, xsrc, xtgt, mats,
    zpk, lpk, field1, field2, rhs, out1, out2, in1, in2,
    tp_send, tp_recv, sp_send, sp_recv, ag1_send, ag1_recv, ag2_send, ag2_recv,
    rs1_send, rs1_recv, rs2_send, rs2_recv,
):
    barrier = pltpu.get_barrier_semaphore()
    for slot in range(n_tgt - 1):
        pl.semaphore_signal(barrier, inc=1, device_id=target_peer(slot), device_id_type=MESH)
    for slot in range(1, n_src):
        pl.semaphore_signal(barrier, inc=1, device_id=source_peer(slot), device_id_type=MESH)

    ptile[...] = jnp.zeros_like(ptile)
    ptile[0:3, 0:own] = pos_ref[...] - middle
    tile = ptile[...]
    tile = tile + pltpu.roll(tile, 64, 1)
    ptile[...] = tile
    tpos[n_tgt - 1] = tile
    spos[0] = tile
    square[...] = jnp.zeros_like(square)
    for a in range(3):
        square[32 * a : 32 * a + 32, 0:own] = noise_ref[a]
    noise = pack(square[...].T[:own])
    zpk[...] = noise
    field1[0] = noise

    pl.semaphore_wait(barrier, n_tgt - 1 + n_src - 1)
    copies = []
    for slot in range(n_src - 1, 0, -1):
        c = remote(ptile, spos.at[slot], sp_send.at[slot], sp_recv.at[slot], source_peer(slot))
        c.start()
        copies.append(c)
    for slot in range(n_tgt - 1):
        there = {1: slot + 4, 2: slot - 4}.get(slot // 4, slot)
        c = remote(ptile, tpos.at[there], tp_send.at[slot], tp_recv.at[there], target_peer(slot))
        c.start()
        copies.append(c)

    def start_gather(block, field, send, recv):
        started = []
        for slot in range(n_src - 1, 0, -1):
            c = remote(block, field.at[slot], send.at[slot], recv.at[slot], source_peer(slot))
            c.start()
            started.append(c)
        return started

    gather1 = start_gather(zpk, field1, ag1_send, ag1_recv)

    lowest = bounds_ref[0]
    highest = bounds_ref[1]
    center = 0.5 * (highest + lowest)
    spread = 0.5 * (highest - lowest)
    q = lanes(8)
    angle = math.pi * (q.astype(F32) + 0.5) / node_count
    cosine = jnp.cos(angle)
    samples = jnp.where(q < node_count, jnp.sqrt(jnp.maximum(center + spread * cosine, 0.0)), 0.0)
    weights = [
        2.0 / node_count * jnp.sum(samples * factor, axis=1, keepdims=True)[0:1]
        for factor in (jnp.ones_like(cosine), cosine, jnp.cos(2.0 * angle))
    ]

    for c in copies:
        c.wait_recv()
    first_half = lanes(8) < own
    for p in range(n_src // 2):
        t = jnp.where(first_half, spos[2 * p], spos[2 * p + 1])
        srow[:, 128 * p : 128 * p + 128] = t
        scol[128 * p : 128 * p + 128, 0:8] = t.T
    for p in range(n_tgt // 2):
        t = jnp.where(first_half, tpos[2 * p], tpos[2 * p + 1])
        tcol[128 * p : 128 * p + 128, 0:8] = t.T

    l16 = lanes(16)

    def pattern(c0, c1, c2, last):
        return jnp.where(l16 < 32, c0, jnp.where(l16 < 64, c1, jnp.where(l16 < 96, c2, last)))

    def source_pattern(step, carry):
        rows = pl.ds(pl.multiple_of(step * 16, 16), 16)
        c = [jnp.broadcast_to(scol[rows, b : b + 1], (16, 128)) for b in range(3)]
        xsrc[rows, :] = pattern(c[0], c[1], c[2], 0.0)
        return carry

    lax.fori_loop(0, J // 16, source_pattern, 0)

    def build(step, carry):
        block = step // 4
        row = (step % 4) * 16
        rows = pl.ds(pl.multiple_of(step * 16, 16), 16)
        c = [jnp.broadcast_to(tcol[rows, b : b + 1], (16, 128)) for b in range(3)]
        xtgt[rows, :] = pattern(c[0], c[1], c[2], -1.0)
        for p in range(J // 128):
            cols = slice(128 * p, 128 * p + 128)
            o = [c[b] - srow[b : b + 1, cols] for b in range(3)]
            squared = o[0] * o[0] + o[1] * o[1] + o[2] * o[2] + soft_core
            inverse = lax.rsqrt(squared)
            inverse2 = inverse * inverse
            near = squared < 4.0
            scalar = jnp.where(near, 1.0 - 0.28125 * (squared * inverse), inverse * (0.75 + 0.5 * inverse2))
            dyadic = inverse * jnp.where(near, 0.09375, inverse2 * (0.75 - 1.5 * inverse2))
            for m, value in enumerate((scalar, dyadic * o[0], dyadic * o[1], dyadic * o[2])):
                high, low = split(value)
                mats[block, pl.ds(pl.multiple_of(m * own + row, 16), 16), cols] = high
                mats[block, pl.ds(pl.multiple_of((4 + m) * own + row, 16), 16), cols] = low
        return carry

    lax.fori_loop(0, n_tgt * 4, build, 0)

    l64 = lanes(own)

    def product(field, gathered, out, into, send, recv):
        for c in gathered:
            c.wait_recv()

        for slot in range(n_src):
            rows = slice(own * slot, own * slot + own)
            u = unpack(field[slot])
            y = u * xsrc[rows, :]
            y = y + pltpu.roll(y, 64, 1)
            y = y + pltpu.roll(y, 32, 1)
            high, low = split(jnp.where(l64 < 96, u, y))
            rhs[rows, 0:128] = high
            rhs[rows, 128:256] = low

        def one_block(slot, carry):
            r = jnp.dot(mats[slot], rhs[...], preferred_element_type=F32)
            r = r[:, 0:128] + r[:, 128:256]
            r = r[: 4 * own] + r[4 * own :]
            x = xtgt[pl.ds(pl.multiple_of(slot * own, own), own), :]
            e = []
            for a in range(3):
                y = r[own * (a + 1) : own * (a + 2)] * x
                e.append(y + pltpu.roll(y, 64, 1))
            here = jnp.where(l64 < 32, e[0], jnp.where(l64 < 64, e[1], e[2]))
            there = jnp.where(l64 < 64, e[0], jnp.where(l64 < 96, e[1], e[2]))
            out[slot] = pack(r[:own] + here + pltpu.roll(there, 96, 1))

            @pl.when(slot < n_tgt - 1)
            def _():
                remote(out.at[slot], into.at[slot], send.at[slot], recv.at[slot], target_peer(slot)).start()

            return carry

        lax.fori_loop(0, n_tgt, one_block, 0)
        total = out[n_tgt - 1]
        for slot in range(n_tgt - 2, -1, -1):
            remote(out.at[slot], into.at[slot], send.at[slot], recv.at[slot], target_peer(slot)).wait_recv()
            total = total + into[slot]
        return total

    def emit(value, store):
        square[0:own, :] = unpack(value)
        turned = square[...].T
        for a in range(3):
            store(a, turned[32 * a : 32 * a + 32, 0:own])

    first = product(field1, gather1, out1, in1, rs1_send, rs1_recv)
    noise = zpk[...]
    linear = (first - center * noise) / spread
    lpk[...] = linear
    field2[0] = linear
    gather2 = start_gather(lpk, field2, ag2_send, ag2_recv)

    def store_first(a, value):
        img_ref[0, a] = value

    emit(first, store_first)

    second = product(field2, gather2, out2, in2, rs2_send, rs2_recv)
    quadratic = 2.0 * (second - center * linear) / spread - noise

    def store_second(a, value):
        img_ref[1, a] = value

    emit(second, store_second)

    def store_disp(a, value):
        disp_ref[a] = value

    emit(0.5 * weights[0] * noise + weights[1] * linear + weights[2] * quadratic, store_disp)

    for c in copies + gather1 + gather2:
        c.wait_send()
    for out, into, send, recv in ((out1, in1, rs1_send, rs1_recv), (out2, in2, rs2_send, rs2_recv)):
        for slot in range(n_tgt - 1):
            remote(out.at[slot], into.at[slot], send.at[slot], recv.at[slot], target_peer(slot)).wait_send()


def body(positions, noise_vectors, spectrum_bounds):
    vmem = pl.BlockSpec(memory_space=pltpu.VMEM)
    dma = pltpu.SemaphoreType.DMA
    return pl.pallas_call(
        body_kernel,
        out_shape=(
            jax.ShapeDtypeStruct((3, 32, own), F32),
            jax.ShapeDtypeStruct((2, 3, 32, own), F32),
        ),
        in_specs=[vmem, vmem, pl.BlockSpec(memory_space=pltpu.SMEM)],
        out_specs=(vmem, vmem),
        scratch_shapes=[
            pltpu.VMEM((128, 128), F32),
            pltpu.VMEM((8, 128), F32),
            pltpu.VMEM((n_tgt, 8, 128), F32),
            pltpu.VMEM((n_src, 8, 128), F32),
            pltpu.VMEM((8, J), F32),
            pltpu.VMEM((J, 128), F32),
            pltpu.VMEM((n_tgt * own, 128), F32),
            pltpu.VMEM((J, 128), F32),
            pltpu.VMEM((n_tgt * own, 128), F32),
            pltpu.VMEM((n_tgt, 8 * own, J), BF16),
            pltpu.VMEM((packed, 128), F32),
            pltpu.VMEM((packed, 128), F32),
            pltpu.VMEM((n_src, packed, 128), F32),
            pltpu.VMEM((n_src, packed, 128), F32),
            pltpu.VMEM((J, 256), BF16),
            pltpu.VMEM((n_tgt, packed, 128), F32),
            pltpu.VMEM((n_tgt, packed, 128), F32),
            pltpu.VMEM((n_tgt, packed, 128), F32),
            pltpu.VMEM((n_tgt, packed, 128), F32),
            dma((n_tgt,)), dma((n_tgt,)), dma((n_src,)), dma((n_src,)),
            dma((n_src,)), dma((n_src,)), dma((n_src,)), dma((n_src,)),
            dma((n_tgt,)), dma((n_tgt,)), dma((n_tgt,)), dma((n_tgt,)),
        ],
        compiler_params=pltpu.CompilerParams(
            collective_id=0, has_side_effects=True, vmem_limit_bytes=40 << 20
        ),
        name="mobility_root",
    )(positions, noise_vectors, spectrum_bounds)


def solution(mesh):
    return jax.shard_map(
        body,
        mesh=mesh,
        in_specs=(P(None, ("blk", "tile")), P(None, None, ("blk", "tile")), P()),
        out_specs=(P(None, None, ("blk", "tile")), P(None, None, None, ("blk", "tile"))),
        check_vma=False,
    )
```

```python
import math

import jax
import jax.numpy as jnp
from jax import lax
from jax.experimental import pallas as pl
from jax.experimental.pallas import tpu as pltpu
from jax.sharding import PartitionSpec as P

MESH = pl.DeviceIdType.MESH
F32 = jnp.float32
BF16 = jnp.bfloat16

soft_core = 1e-06
node_count = 32
edge = (41.9 * 8192) ** (1.0 / 3.0)
middle = 0.5 * edge

own = 64
packed = 48
n_src = 8
n_tgt = 16
J = n_src * own

SOURCES = [(0, 0), (1, 0), (3, 0), (0, 1), (2, 0), (1, 1), (3, 1), (2, 1)]


def coords():
    block = lax.axis_index("blk")
    half = lax.axis_index("tile")
    return block // 16, (block // 8) % 2, (block // 2) % 4, block % 2, half


def source_peer(slot):
    dy, flip = SOURCES[slot]
    y, low, z, core, high = coords()
    return ((((y + dy) % 4) * 2 + (low + flip) % 2) * 4 + z) * 2 + core, high


def target_peer(slot):
    quarter = slot // 4
    dz = (2 + 3 * quarter + (quarter // 2) * (3 + 2 * (quarter % 2))) % 4
    flip = 1 - (slot // 2) % 2
    swap = 1 - slot % 2
    y, low, z, core, high = coords()
    return (
        ((y * 2 + (low + flip) % 2) * 4 + (z + dz) % 4) * 2 + (core + swap) % 2,
        (high + flip) % 2,
    )


def remote(src, dst, send, recv, device):
    return pltpu.make_async_remote_copy(
        src_ref=src, dst_ref=dst, send_sem=send, recv_sem=recv, device_id=device, device_id_type=MESH
    )


def lanes(rows):
    return lax.broadcasted_iota(jnp.int32, (rows, 128), 1)


def pack(full):
    tail = full[packed:own]
    moved = jnp.concatenate([pltpu.roll(tail, 96 - 32 * g, 1) if g < 3 else tail for g in range(3)], axis=0)
    return jnp.where(lanes(packed) < 96, full[:packed], moved)


def unpack(block):
    l16 = lanes(16)
    parts = [pltpu.roll(block[16 * g : 16 * g + 16], 32 + 32 * g, 1) for g in range(3)]
    tail = jnp.where(l16 < 32, parts[0], jnp.where(l16 < 64, parts[1], parts[2]))
    return jnp.concatenate([block, tail], axis=0)


def split(value):
    high = value.astype(BF16)
    low = (value - high.astype(F32)).astype(BF16)
    return high, low


def body_kernel(
    pos_hbm, noise_hbm, bounds_hbm, disp_ref, img_ref,
    pos_ref, noise_ref, bounds_ref, in_sem, square, ptile, tpos, spos, srow, bcol, xsrc, xtgt, mats, raw0, raw1,
    zpk, lpk, field1, field2, rhs, out1, out2, in1, in2,
    tp_send, tp_recv, sp_send, sp_recv, ag1_send, ag1_recv, ag2_send, ag2_recv,
    rs1_send, rs1_recv, rs2_send, rs2_recv,
):
    loads = [
        pltpu.make_async_copy(src, dst, in_sem.at[k])
        for k, (src, dst) in enumerate(((pos_hbm, pos_ref), (noise_hbm, noise_ref), (bounds_hbm, bounds_ref)))
    ]
    for c in loads:
        c.start()
    barrier = pltpu.get_barrier_semaphore()
    for slot in range(n_tgt - 1):
        pl.semaphore_signal(barrier, inc=1, device_id=target_peer(slot), device_id_type=MESH)
    for slot in range(1, n_src):
        pl.semaphore_signal(barrier, inc=1, device_id=source_peer(slot), device_id_type=MESH)

    ptile[...] = jnp.zeros_like(ptile)
    square[...] = jnp.zeros_like(square)
    for c in loads:
        c.wait()
    ptile[0:3, 0:own] = pos_ref[...] - middle
    tile = ptile[...]
    tile = tile + pltpu.roll(tile, 64, 1)
    ptile[...] = tile
    tpos[n_tgt - 1] = tile
    spos[0] = tile
    for a in range(3):
        square[32 * a : 32 * a + 32, 0:own] = noise_ref[a]
    noise = pack(square[...].T[:own])
    zpk[...] = noise
    field1[0] = noise

    pl.semaphore_wait(barrier, n_tgt - 1 + n_src - 1)
    copies = []
    for slot in range(n_src - 1, 0, -1):
        c = remote(ptile, spos.at[slot], sp_send.at[slot], sp_recv.at[slot], source_peer(slot))
        c.start()
        copies.append(c)
    for slot in range(n_tgt - 1):
        there = {1: slot + 4, 2: slot - 4}.get(slot // 4, slot)
        c = remote(ptile, tpos.at[there], tp_send.at[slot], tp_recv.at[there], target_peer(slot))
        c.start()
        copies.append(c)

    def start_gather(block, field, send, recv):
        started = {}
        for slot in range(n_src - 1, 0, -1):
            c = remote(block, field.at[slot], send.at[slot], recv.at[slot], source_peer(slot))
            c.start()
            started[slot] = c
        return started

    gather1 = start_gather(zpk, field1, ag1_send, ag1_recv)

    lowest = bounds_ref[0]
    highest = bounds_ref[1]
    center = 0.5 * (highest + lowest)
    spread = 0.5 * (highest - lowest)
    q = lanes(8)
    angle = math.pi * (q.astype(F32) + 0.5) / node_count
    cosine = jnp.cos(angle)
    samples = jnp.where(q < node_count, jnp.sqrt(jnp.maximum(center + spread * cosine, 0.0)), 0.0)
    weights = [
        2.0 / node_count * jnp.sum(samples * factor, axis=1, keepdims=True)[0:1]
        for factor in (jnp.ones_like(cosine), cosine, jnp.cos(2.0 * angle))
    ]

    def pattern(c0, c1, c2, last):
        lane = lanes(c0.shape[0])
        return jnp.where(lane < 32, c0, jnp.where(lane < 64, c1, jnp.where(lane < 96, c2, last)))

    for c in copies:
        c.wait_recv()
    first_half = lanes(8) < own
    for p in range(n_src // 2):
        t = jnp.where(first_half, spos[2 * p], spos[2 * p + 1])
        srow[:, 128 * p : 128 * p + 128] = t
        turned = t.T
        c = [jnp.broadcast_to(turned[:, b : b + 1], (128, 128)) for b in range(3)]
        xsrc[128 * p : 128 * p + 128, :] = pattern(*c, 0.0)
    for p in range(n_tgt // 2):
        t = jnp.where(first_half, tpos[2 * p], tpos[2 * p + 1])
        turned = t.T
        c = [jnp.broadcast_to(turned[:, b : b + 1], (128, 128)) for b in range(3)]
        for b in range(3):
            bcol[b, 128 * p : 128 * p + 128, :] = c[b]
        xtgt[128 * p : 128 * p + 128, :] = pattern(*c, -1.0)

    def build(pair, carry):
        for row in range(0, 2 * own, 16):
            rows = pl.ds(pl.multiple_of(pair * 2 * own + row, 16), 16)
            c = [bcol[b, rows, :] for b in range(3)]
            for p in range(J // 128):
                cols = slice(128 * p, 128 * p + 128)
                o = [c[b] - srow[b : b + 1, cols] for b in range(3)]
                squared = o[0] * o[0] + o[1] * o[1] + o[2] * o[2] + soft_core
                inverse = lax.rsqrt(squared)
                inverse2 = inverse * inverse
                near = squared < 4.0
                scalar = jnp.where(near, 1.0 - 0.28125 * (squared * inverse), inverse * (0.75 + 0.5 * inverse2))
                dyadic = inverse * jnp.where(near, 0.09375, inverse2 * (0.75 - 1.5 * inverse2))
                for m, value in enumerate((scalar, dyadic * o[0], dyadic * o[1], dyadic * o[2])):
                    high, low = split(value)
                    at = (row // own * 4 + m) * own + row % own
                    mats[pair, at : at + 16, cols] = high
                    mats[pair, at : at + 16, J + 128 * p : J + 128 * p + 128] = low
        return carry

    lax.fori_loop(0, n_tgt // 2, build, 0)

    raw = (raw0, raw1)
    l64 = lanes(own)

    def product(field, gathered, out, into, send, recv):
        for slot in range(n_src):
            if slot:
                gathered[slot].wait_recv()
            rows = slice(own * slot, own * slot + own)
            u = unpack(field[slot])
            y = u * xsrc[rows, :]
            y = y + pltpu.roll(y, 64, 1)
            y = y + pltpu.roll(y, 32, 1)
            high, low = split(jnp.where(l64 < 96, u, y))
            for at in (own * slot, J + own * slot):
                rhs[at : at + own, 0:128] = high
                rhs[at : at + own, 128:256] = low

        def multiply(pair):
            raw[pair % 2][...] = jnp.dot(mats[pair], rhs[...], preferred_element_type=F32)

        lane = lanes(16)

        def rows_of(source, slot, base, g):
            at = slot * own + 16 * g
            x = xtgt[at : at + 16, :]
            r = []
            for m in range(4):
                rows = slice(base + own * m + 16 * g, base + own * m + 16 * g + 16)
                r.append(source[rows, 0:128] + source[rows, 128:256])
            e = [r[m] * x for m in (1, 2, 3)]
            e = [v + pltpu.roll(v, 64, 1) for v in e]
            here = jnp.where(lane < 32, e[0], jnp.where(lane < 64, e[1], e[2]))
            there = jnp.where(lane < 64, e[0], jnp.where(lane < 96, e[1], e[2]))
            return r[0] + here + pltpu.roll(there, 96, 1)

        def combine(pair):
            for half in range(2):
                slot = 2 * pair + half
                base = half * 4 * own
                tail = rows_of(raw[pair % 2], slot, base, 3)
                for g in range(3):
                    out[slot, 16 * g : 16 * g + 16, :] = jnp.where(
                        lane < 96, rows_of(raw[pair % 2], slot, base, g), pltpu.roll(tail, 96 - 32 * g, 1)
                    )
                if slot < n_tgt - 1:
                    remote(out.at[slot], into.at[slot], send.at[slot], recv.at[slot], target_peer(slot)).start()

        multiply(0)
        for pair in range(1, n_tgt // 2):
            multiply(pair)
            combine(pair - 1)
        combine(n_tgt // 2 - 1)
        total = out[n_tgt - 1]
        for slot in range(n_tgt - 2, -1, -1):
            remote(out.at[slot], into.at[slot], send.at[slot], recv.at[slot], target_peer(slot)).wait_recv()
            total = total + into[slot]
        return total

    def emit(value, store):
        square[0:own, :] = unpack(value)
        turned = square[...].T
        for a in range(3):
            store(a, turned[32 * a : 32 * a + 32, 0:own])

    first = product(field1, gather1, out1, in1, rs1_send, rs1_recv)
    noise = zpk[...]
    linear = (first - center * noise) / spread
    lpk[...] = linear
    field2[0] = linear
    gather2 = start_gather(lpk, field2, ag2_send, ag2_recv)

    def store_first(a, value):
        img_ref[0, a] = value

    emit(first, store_first)

    second = product(field2, gather2, out2, in2, rs2_send, rs2_recv)
    quadratic = 2.0 * (second - center * linear) / spread - noise

    def store_second(a, value):
        img_ref[1, a] = value

    emit(second, store_second)

    def store_disp(a, value):
        disp_ref[a] = value

    emit(0.5 * weights[0] * noise + weights[1] * linear + weights[2] * quadratic, store_disp)

    for c in copies + list(gather1.values()) + list(gather2.values()):
        c.wait_send()
    for out, into, send, recv in ((out1, in1, rs1_send, rs1_recv), (out2, in2, rs2_send, rs2_recv)):
        for slot in range(n_tgt - 1):
            remote(out.at[slot], into.at[slot], send.at[slot], recv.at[slot], target_peer(slot)).wait_send()


def body(positions, noise_vectors, spectrum_bounds):
    vmem = pl.BlockSpec(memory_space=pltpu.VMEM)
    dma = pltpu.SemaphoreType.DMA
    return pl.pallas_call(
        body_kernel,
        out_shape=(
            jax.ShapeDtypeStruct((3, 32, own), F32),
            jax.ShapeDtypeStruct((2, 3, 32, own), F32),
        ),
        in_specs=[pl.BlockSpec(memory_space=pl.ANY)] * 3,
        out_specs=(vmem, vmem),
        scratch_shapes=[
            pltpu.VMEM((3, own), F32),
            pltpu.VMEM((3, 32, own), F32),
            pltpu.SMEM((2,), F32),
            dma((3,)),
            pltpu.VMEM((128, 128), F32),
            pltpu.VMEM((8, 128), F32),
            pltpu.VMEM((n_tgt, 8, 128), F32),
            pltpu.VMEM((n_src, 8, 128), F32),
            pltpu.VMEM((8, J), F32),
            pltpu.VMEM((3, n_tgt * own, 128), F32),
            pltpu.VMEM((J, 128), F32),
            pltpu.VMEM((n_tgt * own, 128), F32),
            pltpu.VMEM((n_tgt // 2, 8 * own, 2 * J), BF16),
            pltpu.VMEM((8 * own, 256), F32),
            pltpu.VMEM((8 * own, 256), F32),
            pltpu.VMEM((packed, 128), F32),
            pltpu.VMEM((packed, 128), F32),
            pltpu.VMEM((n_src, packed, 128), F32),
            pltpu.VMEM((n_src, packed, 128), F32),
            pltpu.VMEM((2 * J, 256), BF16),
            pltpu.VMEM((n_tgt, packed, 128), F32),
            pltpu.VMEM((n_tgt, packed, 128), F32),
            pltpu.VMEM((n_tgt, packed, 128), F32),
            pltpu.VMEM((n_tgt, packed, 128), F32),
            dma((n_tgt,)), dma((n_tgt,)), dma((n_src,)), dma((n_src,)),
            dma((n_src,)), dma((n_src,)), dma((n_src,)), dma((n_src,)),
            dma((n_tgt,)), dma((n_tgt,)), dma((n_tgt,)), dma((n_tgt,)),
        ],
        compiler_params=pltpu.CompilerParams(
            collective_id=0, has_side_effects=True, vmem_limit_bytes=40 << 20
        ),
        name="mobility_root",
    )(positions, noise_vectors, spectrum_bounds)


def solution(mesh):
    return jax.shard_map(
        body,
        mesh=mesh,
        in_specs=(P(None, ("blk", "tile")), P(None, None, ("blk", "tile")), P()),
        out_specs=(P(None, None, ("blk", "tile")), P(None, None, None, ("blk", "tile"))),
        check_vma=False,
    )
```

```python
import math

import jax
import jax.numpy as jnp
from jax import lax
from jax.experimental import pallas as pl
from jax.experimental.pallas import tpu as pltpu
from jax.sharding import PartitionSpec as P

MESH = pl.DeviceIdType.MESH
F32 = jnp.float32
BF16 = jnp.bfloat16

soft_core = 1e-06
node_count = 32
edge = (41.9 * 8192) ** (1.0 / 3.0)
middle = 0.5 * edge

own = 64
packed = 48
n_src = 8
n_tgt = 16
n_pair = n_tgt // 2
J = n_src * own

SOURCES = [(0, 0), (1, 0), (3, 0), (0, 1), (2, 0), (1, 1), (3, 1), (2, 1)]


def coords():
    block = lax.axis_index("blk")
    half = lax.axis_index("tile")
    return block // 16, (block // 8) % 2, (block // 2) % 4, block % 2, half


def source_peer(slot):
    dy, flip = SOURCES[slot]
    y, low, z, core, high = coords()
    return ((((y + dy) % 4) * 2 + (low + flip) % 2) * 4 + z) * 2 + core, high


TARGETS = [(2, 1), (2, 0), (1, 1), (3, 1), (1, 0), (3, 0), (0, 1), (0, 0)]
BACK = [0, 1, 3, 2, 5, 4, 6, 7]


def target_peer(slot):
    dz, flip = TARGETS[slot % n_pair]
    swap = 1 - slot // n_pair
    y, low, z, core, high = coords()
    return (
        ((y * 2 + (low + flip) % 2) * 4 + (z + dz) % 4) * 2 + (core + swap) % 2,
        (high + flip) % 2,
    )


def remote(src, dst, send, recv, device):
    return pltpu.make_async_remote_copy(
        src_ref=src, dst_ref=dst, send_sem=send, recv_sem=recv, device_id=device, device_id_type=MESH
    )


def lanes(rows):
    return lax.broadcasted_iota(jnp.int32, (rows, 128), 1)


def pack(full):
    tail = full[packed:own]
    moved = jnp.concatenate([pltpu.roll(tail, 96 - 32 * g, 1) if g < 3 else tail for g in range(3)], axis=0)
    return jnp.where(lanes(packed) < 96, full[:packed], moved)


def unpack(block):
    l16 = lanes(16)
    parts = [pltpu.roll(block[16 * g : 16 * g + 16], 32 + 32 * g, 1) for g in range(3)]
    tail = jnp.where(l16 < 32, parts[0], jnp.where(l16 < 64, parts[1], parts[2]))
    return jnp.concatenate([block, tail], axis=0)


def split(value):
    high = value.astype(BF16)
    low = (value - high.astype(F32)).astype(BF16)
    return high, low


def body_kernel(
    pos_hbm, noise_hbm, bounds_hbm, disp_ref, img_ref,
    pos_ref, noise_ref, bounds_ref, in_sem, square, ptile, tpos, spos, srow, bcol, xsrc, xtgt, mats, raw0, raw1,
    zpk, lpk, field, rhs, mine, other, into, totals,
    tp_send, tp_recv, sp_send, sp_recv, ag_send, ag_recv, sb_send, sb_recv, rs_send, rs_recv,
):
    loads = [
        pltpu.make_async_copy(src, dst, in_sem.at[k])
        for k, (src, dst) in enumerate(((pos_hbm, pos_ref), (noise_hbm, noise_ref), (bounds_hbm, bounds_ref)))
    ]
    for c in loads:
        c.start()
    barrier = pltpu.get_barrier_semaphore()
    for slot in range(n_tgt - 1):
        pl.semaphore_signal(barrier, inc=1, device_id=target_peer(slot), device_id_type=MESH)
    for slot in range(1, n_src):
        pl.semaphore_signal(barrier, inc=1, device_id=source_peer(slot), device_id_type=MESH)

    ptile[...] = jnp.zeros_like(ptile)
    square[...] = jnp.zeros_like(square)
    for c in loads:
        c.wait()
    ptile[0:3, 0:own] = pos_ref[...] - middle
    tile = ptile[...]
    tile = tile + pltpu.roll(tile, 64, 1)
    ptile[...] = tile
    tpos[n_tgt - 1] = tile
    spos[0] = tile
    for a in range(3):
        square[32 * a : 32 * a + 32, 0:own] = noise_ref[a]
    noise = pack(square[...].T[:own])
    zpk[...] = noise
    field[1, 0] = noise

    raw = (raw0, raw1)
    l64 = lanes(own)

    lane = lanes(16)

    def rows_of(source, slot, base, g):
        x = xtgt[pl.ds(pl.multiple_of(slot * own + 16 * g, 16), 16), :]
        r = []
        for m in range(4):
            rows = slice(base + own * m + 16 * g, base + own * m + 16 * g + 16)
            r.append(source[rows, 0:128] + source[rows, 128:256])
        e = [r[m] * x for m in (1, 2, 3)]
        e = [v + pltpu.roll(v, 64, 1) for v in e]
        here = jnp.where(lane < 32, e[0], jnp.where(lane < 64, e[1], e[2]))
        there = jnp.where(lane < 64, e[0], jnp.where(lane < 96, e[1], e[2]))
        return r[0] + here + pltpu.roll(there, 96, 1)

    def emit(value, store):
        square[0:own, :] = unpack(value)
        turned = square[...].T
        for a in range(3):
            store(a, turned[32 * a : 32 * a + 32, 0:own])

    def gather(phase, block):
        return [
            remote(block, field.at[phase, slot], ag_send.at[phase, slot], ag_recv.at[phase, slot], source_peer(slot))
            for slot in range(n_src - 1, 0, -1)
        ]

    pl.semaphore_wait(barrier, n_tgt - 1 + n_src - 1)
    spread_pos, target_pos = {}, {}
    for slot in range(n_src - 1, 0, -1):
        c = remote(ptile, spos.at[slot], sp_send.at[slot], sp_recv.at[slot], source_peer(slot))
        c.start()
        spread_pos[slot] = c
    for slot in range(n_tgt - 1):
        there = slot // n_pair * n_pair + BACK[slot % n_pair]
        c = remote(ptile, tpos.at[there], tp_send.at[slot], tp_recv.at[there], target_peer(slot))
        c.start()
        target_pos[there] = c

    for c in gather(1, zpk):
        c.start()

    lowest = bounds_ref[0]
    highest = bounds_ref[1]
    center = 0.5 * (highest + lowest)
    spread = 0.5 * (highest - lowest)
    q = lanes(8)
    angle = math.pi * (q.astype(F32) + 0.5) / node_count
    cosine = jnp.cos(angle)
    samples = jnp.where(q < node_count, jnp.sqrt(jnp.maximum(center + spread * cosine, 0.0)), 0.0)
    weights = [
        2.0 / node_count * jnp.sum(samples * factor, axis=1, keepdims=True)[0:1]
        for factor in (jnp.ones_like(cosine), cosine, jnp.cos(2.0 * angle))
    ]

    def pattern(c0, c1, c2, last):
        lane = lanes(c0.shape[0])
        return jnp.where(lane < 32, c0, jnp.where(lane < 64, c1, jnp.where(lane < 96, c2, last)))

    def startup():
        first_half = lanes(8) < own

        def columns(tile):
            turned = tile.T
            return [jnp.broadcast_to(turned[:, b : b + 1], (128, 128)) for b in range(3)]

        def take_source(p):
            for slot in (2 * p, 2 * p + 1):
                if slot:
                    spread_pos[slot].wait_recv()
            tile = jnp.where(first_half, spos[2 * p], spos[2 * p + 1])
            srow[:, 128 * p : 128 * p + 128] = tile
            xsrc[128 * p : 128 * p + 128, :] = pattern(*columns(tile), 0.0)

        def take_target(p):
            for slot in (2 * p, 2 * p + 1):
                if slot < n_tgt - 1:
                    target_pos[slot].wait_recv()
            c = columns(jnp.where(first_half, tpos[2 * p], tpos[2 * p + 1]))
            for b in range(3):
                bcol[b, 128 * p : 128 * p + 128, :] = c[b]
            xtgt[128 * p : 128 * p + 128, :] = pattern(*c, -1.0)

        def build(choose):
            def body(step, carry):
                pair, half = choose(step)
                for row in range(0, 2 * own, 16):
                    rows = pl.ds(pl.multiple_of(pair * 2 * own + row, 16), 16)
                    c = [bcol[b, rows, :] for b in range(3)]
                    for p in range(2):
                        first = pl.multiple_of(half * 256 + 128 * p, 128)
                        cols = pl.ds(first, 128)
                        o = [c[b] - srow[b : b + 1, cols] for b in range(3)]
                        squared = o[0] * o[0] + o[1] * o[1] + o[2] * o[2] + soft_core
                        inverse = lax.rsqrt(squared)
                        inverse2 = inverse * inverse
                        near = squared < 4.0
                        scalar = jnp.where(near, 1.0 - 0.28125 * (squared * inverse), inverse * (0.75 + 0.5 * inverse2))
                        dyadic = inverse * jnp.where(near, 0.09375, inverse2 * (0.75 - 1.5 * inverse2))
                        for m, value in enumerate((scalar, dyadic * o[0], dyadic * o[1], dyadic * o[2])):
                            high, low = split(value)
                            at = (row // own * 4 + m) * own + row % own
                            mats[pair, at : at + 16, cols] = high
                            mats[pair, at : at + 16, pl.ds(pl.multiple_of(J + first, 128), 128)] = low
                return carry

            return body

        for p in (0, 1):
            take_source(p)
        for p in (7, 3, 6, 2):
            take_target(p)
        lax.fori_loop(0, 4, build(lambda step: (step // 2 * 4 + 2 + step % 2, 0)), 0)
        for p in (2, 3):
            take_source(p)
        for p in (5, 4, 1, 0):
            take_target(p)
        lax.fori_loop(0, 12, build(lambda step: (step - step // 8 * (8 - (step - 8) // 2 * 2), 1 - step // 8)), 0)

        for c in list(spread_pos.values()) + list(target_pos.values()):
            c.wait_send()

    def to_sibling(phase, quarter):
        some = pl.ds(quarter * 4, 4)
        return remote(
            mine.at[phase, some], other.at[phase, some], sb_send.at[phase, quarter], sb_recv.at[phase, quarter],
            target_peer(n_pair - 1),
        )

    def to_owner(phase, chip):
        return remote(
            mine.at[phase, n_pair + chip], into.at[phase, chip], rs_send.at[phase, chip], rs_recv.at[phase, chip],
            target_peer(n_pair + chip),
        )

    def one_phase(phase, carry):
        pl.when(phase == 1)(startup)

        def fields_of(slots):
            @pl.when(phase > 0)
            def _():
                for slot, c in zip(range(n_src - 1, 0, -1), gather(phase, zpk)):
                    if slot in slots:
                        c.wait_recv()

            for slot in slots:
                rows = slice(own * slot, own * slot + own)
                u = unpack(field[phase, slot])
                y = u * xsrc[rows, :]
                y = y + pltpu.roll(y, 64, 1)
                y = y + pltpu.roll(y, 32, 1)
                high, low = split(jnp.where(l64 < 96, u, y))
                for at in (own * slot, J + own * slot):
                    rhs[at : at + own, 0:128] = high
                    rhs[at : at + own, 128:256] = low

        fields_of(range(4))
        fields_of(range(4, n_src))

        def multiply(pair, place):
            raw[place][...] = jnp.dot(mats[pair], rhs[...], preferred_element_type=F32)

        def combine(pair, place):
            for half in range(2):
                slot = 2 * pair + half
                base = half * 4 * own
                tail = rows_of(raw[place], slot, base, 3)
                for g in range(3):
                    mine[phase, slot, 16 * g : 16 * g + 16, :] = jnp.where(
                        lane < 96, rows_of(raw[place], slot, base, g), pltpu.roll(tail, 96 - 32 * g, 1)
                    )

        def quarter_of(quarter, carry):
            multiply(2 * quarter, 0)
            multiply(2 * quarter + 1, 1)
            combine(2 * quarter, 0)
            combine(2 * quarter + 1, 1)
            for q in range(2):

                @pl.when((phase > 0) & (quarter == q))
                def _():
                    to_sibling(phase, q).start()

                @pl.when((phase > 0) & (quarter == q + 2))
                def _():
                    to_sibling(phase, q).wait_recv()
                    for chip in range(4 * q, 4 * q + 4):
                        mine[phase, n_pair + chip] = mine[phase, n_pair + chip] + other[phase, chip]
                        if chip < n_pair - 1:
                            to_owner(phase, chip).start()

            return carry

        lax.fori_loop(0, 4, quarter_of, 0)

        @pl.when(phase > 0)
        def _():
            for chip in range(n_pair - 1):
                to_owner(phase, chip).wait_recv()

        total = mine[phase, n_tgt - 1]
        for chip in range(n_pair - 1):
            total = total + into[phase, chip]
        totals[...] = total

        @pl.when(phase == 1)
        def _():
            linear = (total - center * zpk[...]) / spread
            lpk[...] = linear
            field[2, 0] = linear
            for c in gather(2, lpk):
                c.start()

        def store_image(a, value):
            img_ref[phase // 2, a] = value

        emit(total, store_image)

        @pl.when(phase > 0)
        def _():
            for q in range(2):
                to_sibling(phase, q).wait_send()
            for chip in range(n_pair - 1):
                to_owner(phase, chip).wait_send()

        return carry

    lax.fori_loop(1, 3, one_phase, 0)
    noise = zpk[...]
    linear = lpk[...]
    quadratic = 2.0 * (totals[...] - center * linear) / spread - noise

    def store_disp(a, value):
        disp_ref[a] = value

    emit(0.5 * weights[0] * noise + weights[1] * linear + weights[2] * quadratic, store_disp)
    for c in gather(1, zpk) + gather(2, lpk):
        c.wait_send()


def body(positions, noise_vectors, spectrum_bounds):
    vmem = pl.BlockSpec(memory_space=pltpu.VMEM)
    dma = pltpu.SemaphoreType.DMA
    return pl.pallas_call(
        body_kernel,
        out_shape=(
            jax.ShapeDtypeStruct((3, 32, own), F32),
            jax.ShapeDtypeStruct((2, 3, 32, own), F32),
        ),
        in_specs=[pl.BlockSpec(memory_space=pltpu.HBM)] * 3,
        out_specs=(vmem, vmem),
        scratch_shapes=[
            pltpu.VMEM((3, own), F32),
            pltpu.VMEM((3, 32, own), F32),
            pltpu.SMEM((2,), F32),
            dma((3,)),
            pltpu.VMEM((128, 128), F32),
            pltpu.VMEM((8, 128), F32),
            pltpu.VMEM((n_tgt, 8, 128), F32),
            pltpu.VMEM((n_src, 8, 128), F32),
            pltpu.VMEM((8, J), F32),
            pltpu.VMEM((3, n_tgt * own, 128), F32),
            pltpu.VMEM((J, 128), F32),
            pltpu.VMEM((n_tgt * own, 128), F32),
            pltpu.VMEM((n_tgt // 2, 8 * own, 2 * J), BF16),
            pltpu.VMEM((8 * own, 256), F32),
            pltpu.VMEM((8 * own, 256), F32),
            pltpu.VMEM((packed, 128), F32),
            pltpu.VMEM((packed, 128), F32),
            pltpu.VMEM((3, n_src, packed, 128), F32),
            pltpu.VMEM((2 * J, 256), BF16),
            pltpu.VMEM((3, n_tgt, packed, 128), F32),
            pltpu.VMEM((3, n_pair, packed, 128), F32),
            pltpu.VMEM((3, n_pair, packed, 128), F32),
            pltpu.VMEM((packed, 128), F32),
            dma((n_tgt,)), dma((n_tgt,)), dma((n_src,)), dma((n_src,)),
            dma((3, n_src)), dma((3, n_src)), dma((3, 2)), dma((3, 2)),
            dma((3, n_pair)), dma((3, n_pair)),
        ],
        compiler_params=pltpu.CompilerParams(
            collective_id=0, has_side_effects=True, vmem_limit_bytes=64 << 20
        ),
        name="mobility_root",
    )(positions, noise_vectors, spectrum_bounds)


def solution(mesh):
    return jax.shard_map(
        body,
        mesh=mesh,
        in_specs=(P(None, ("blk", "tile")), P(None, None, ("blk", "tile")), P()),
        out_specs=(P(None, None, ("blk", "tile")), P(None, None, None, ("blk", "tile"))),
        check_vma=False,
    )
```

```python
import math

import jax
import jax.numpy as jnp
from jax import lax
from jax.experimental import pallas as pl
from jax.experimental.pallas import tpu as pltpu
from jax.sharding import PartitionSpec as P

MESH = pl.DeviceIdType.MESH
F32 = jnp.float32
BF16 = jnp.bfloat16

soft_core = 1e-06
node_count = 32
edge = (41.9 * 8192) ** (1.0 / 3.0)
middle = 0.5 * edge

own = 64
packed = 48
n_src = 8
n_tgt = 16
n_pair = n_tgt // 2
J = n_src * own

SOURCES = [(0, 0), (1, 0), (3, 0), (0, 1), (2, 0), (1, 1), (3, 1), (2, 1)]


def coords():
    block = lax.axis_index("blk")
    half = lax.axis_index("tile")
    return block // 16, (block // 8) % 2, (block // 2) % 4, block % 2, half


def source_peer(slot):
    dy, flip = SOURCES[slot]
    y, low, z, core, high = coords()
    return ((((y + dy) % 4) * 2 + (low + flip) % 2) * 4 + z) * 2 + core, high


TARGETS = [(2, 1), (2, 0), (1, 1), (3, 1), (1, 0), (3, 0), (0, 1), (0, 0)]
BACK = [0, 1, 3, 2, 5, 4, 6, 7]


def target_peer(slot):
    dz, flip = TARGETS[slot % n_pair]
    swap = 1 - slot // n_pair
    y, low, z, core, high = coords()
    return (
        ((y * 2 + (low + flip) % 2) * 4 + (z + dz) % 4) * 2 + (core + swap) % 2,
        (high + flip) % 2,
    )


def remote(src, dst, send, recv, device):
    return pltpu.make_async_remote_copy(
        src_ref=src, dst_ref=dst, send_sem=send, recv_sem=recv, device_id=device, device_id_type=MESH
    )


def lanes(rows):
    return lax.broadcasted_iota(jnp.int32, (rows, 128), 1)


def pack(full):
    tail = full[packed:own]
    moved = jnp.concatenate([pltpu.roll(tail, 96 - 32 * g, 1) if g < 3 else tail for g in range(3)], axis=0)
    return jnp.where(lanes(packed) < 96, full[:packed], moved)


def unpack(block):
    l16 = lanes(16)
    parts = [pltpu.roll(block[16 * g : 16 * g + 16], 32 + 32 * g, 1) for g in range(3)]
    tail = jnp.where(l16 < 32, parts[0], jnp.where(l16 < 64, parts[1], parts[2]))
    return jnp.concatenate([block, tail], axis=0)


def split(value):
    high = value.astype(BF16)
    low = (value - high.astype(F32)).astype(BF16)
    return high, low


def body_kernel(
    pos_hbm, noise_hbm, bounds_hbm, disp_ref, img_ref,
    pos_ref, noise_ref, bounds_ref, in_sem, square, ptile, tpos, spos, srow, bcol, xsrc, xtgt, mats, raw0, raw1,
    zpk, lpk, field, rhs, mine, other, into, totals,
    tp_send, tp_recv, sp_send, sp_recv, ag_send, ag_recv, sb_send, sb_recv, rs_send, rs_recv,
):
    loads = [
        pltpu.make_async_copy(src, dst, in_sem.at[k])
        for k, (src, dst) in enumerate(((pos_hbm, pos_ref), (noise_hbm, noise_ref), (bounds_hbm, bounds_ref)))
    ]
    for c in loads:
        c.start()
    barrier = pltpu.get_barrier_semaphore()
    for slot in range(n_tgt - 1):
        pl.semaphore_signal(barrier, inc=1, device_id=target_peer(slot), device_id_type=MESH)
    for slot in range(1, n_src):
        pl.semaphore_signal(barrier, inc=1, device_id=source_peer(slot), device_id_type=MESH)

    ptile[...] = jnp.zeros_like(ptile)
    square[...] = jnp.zeros_like(square)
    for c in loads:
        c.wait()
    ptile[0:3, 0:own] = pos_ref[...] - middle
    tile = ptile[...]
    tile = tile + pltpu.roll(tile, 64, 1)
    ptile[...] = tile
    tpos[n_tgt - 1] = tile
    spos[0] = tile
    for a in range(3):
        square[32 * a : 32 * a + 32, 0:own] = noise_ref[a]
    noise = pack(square[...].T[:own])
    zpk[...] = noise
    field[1, 0] = noise

    raw = (raw0, raw1)
    l64 = lanes(own)

    lane = lanes(16)

    def rows_of(source, slot, base, g):
        x = xtgt[pl.ds(pl.multiple_of(slot * own + 16 * g, 16), 16), :]
        r = []
        for m in range(4):
            rows = slice(base + own * m + 16 * g, base + own * m + 16 * g + 16)
            r.append(source[rows, 0:128] + source[rows, 128:256])
        e = [r[m] * x for m in (1, 2, 3)]
        e = [v + pltpu.roll(v, 64, 1) for v in e]
        here = jnp.where(lane < 32, e[0], jnp.where(lane < 64, e[1], e[2]))
        there = jnp.where(lane < 64, e[0], jnp.where(lane < 96, e[1], e[2]))
        return 0.5 * r[0] + here + pltpu.roll(there, 96, 1)

    def emit(value, store):
        square[0:own, :] = unpack(value)
        turned = square[...].T
        for a in range(3):
            store(a, turned[32 * a : 32 * a + 32, 0:own])

    def gather(phase, block):
        return [
            remote(block, field.at[phase, slot], ag_send.at[phase, slot], ag_recv.at[phase, slot], source_peer(slot))
            for slot in range(n_src - 1, 0, -1)
        ]

    pl.semaphore_wait(barrier, n_tgt - 1 + n_src - 1)
    spread_pos, target_pos = {}, {}
    for slot in range(n_src - 1, 0, -1):
        c = remote(ptile, spos.at[slot], sp_send.at[slot], sp_recv.at[slot], source_peer(slot))
        c.start()
        spread_pos[slot] = c
    for slot in range(n_tgt - 1):
        there = slot // n_pair * n_pair + BACK[slot % n_pair]
        c = remote(ptile, tpos.at[there], tp_send.at[slot], tp_recv.at[there], target_peer(slot))
        c.start()
        target_pos[there] = c

    for c in gather(1, zpk):
        c.start()

    lowest = bounds_ref[0]
    highest = bounds_ref[1]
    center = 0.5 * (highest + lowest)
    spread = 0.5 * (highest - lowest)
    q = lanes(8)
    angle = math.pi * (q.astype(F32) + 0.5) / node_count
    cosine = jnp.cos(angle)
    samples = jnp.where(q < node_count, jnp.sqrt(jnp.maximum(center + spread * cosine, 0.0)), 0.0)
    weights = [
        2.0 / node_count * jnp.sum(samples * factor, axis=1, keepdims=True)[0:1]
        for factor in (jnp.ones_like(cosine), cosine, jnp.cos(2.0 * angle))
    ]

    def pattern(c0, c1, c2, last):
        lane = lanes(c0.shape[0])
        return jnp.where(lane < 32, c0, jnp.where(lane < 64, c1, jnp.where(lane < 96, c2, last)))

    def fill(pair, row, count, p):
        rows = pl.ds(pair * 2 * own + row, count)
        c = [bcol[b, rows, :] for b in range(3)]
        cols = slice(128 * p, 128 * p + 128)
        o = [c[b] - srow[b : b + 1, cols] for b in range(3)]
        squared = o[0] * o[0] + o[1] * o[1] + o[2] * o[2] + soft_core
        inverse = lax.rsqrt(squared)
        inverse2 = inverse * inverse
        near = squared < 4.0
        scalar = jnp.where(near, 2.0 - 0.5625 * (squared * inverse), inverse * (1.5 + inverse2))
        dyadic = inverse * jnp.where(near, 0.0625, inverse2 * (0.5 - inverse2))
        for m, value in enumerate((scalar, dyadic * o[0], dyadic * o[1], dyadic * o[2])):
            high, low = split(value)
            at = (row // own * 4 + m) * own + row % own
            mats[pair, at : at + count, cols] = high
            mats[pair, at : at + count, J + 128 * p : J + 128 * p + 128] = low

    def near_tiles(step, carry):
        for row in range(0, 2 * own, 64):
            for p in (0, 1):
                fill(step // 2 * 4 + 2 + step % 2, row, 64, p)
        return carry

    def other_tiles(pair):
        for row in range(0, 2 * own, 64):
            for p in (range(4) if pair % 4 < 2 else (2, 3)):
                fill(pair, row, 64, p)

    def startup():
        first_half = lanes(8) < own

        def columns(tile):
            turned = tile.T
            return [jnp.broadcast_to(turned[:, b : b + 1], (128, 128)) for b in range(3)]

        def take_source(p):
            for slot in (2 * p, 2 * p + 1):
                if slot:
                    spread_pos[slot].wait_recv()
            tile = jnp.where(first_half, spos[2 * p], spos[2 * p + 1])
            srow[:, 128 * p : 128 * p + 128] = tile
            xsrc[128 * p : 128 * p + 128, :] = pattern(*columns(tile), 0.0)

        def take_target(p):
            for slot in (2 * p, 2 * p + 1):
                if slot < n_tgt - 1:
                    target_pos[slot].wait_recv()
            c = columns(jnp.where(first_half, tpos[2 * p], tpos[2 * p + 1]))
            for b in range(3):
                bcol[b, 128 * p : 128 * p + 128, :] = c[b]
            xtgt[128 * p : 128 * p + 128, :] = 1.5 * pattern(*c, -1.0)

        for p in (0, 1):
            take_source(p)
        for p in (7, 3, 6, 2):
            take_target(p)
        lax.fori_loop(0, 4, near_tiles, 0)
        for p in (2, 3):
            take_source(p)
        for p in (5, 4, 1, 0):
            take_target(p)

        for c in list(spread_pos.values()) + list(target_pos.values()):
            c.wait_send()

    def to_sibling(phase, quarter):
        some = pl.ds(quarter * 4, 4)
        return remote(
            mine.at[phase, some], other.at[phase, some], sb_send.at[phase, quarter], sb_recv.at[phase, quarter],
            target_peer(n_pair - 1),
        )

    def to_owner(phase, chip):
        return remote(
            mine.at[phase, n_pair + chip], into.at[phase, chip], rs_send.at[phase, chip], rs_recv.at[phase, chip],
            target_peer(n_pair + chip),
        )

    def one_phase(phase, carry):
        def fields_of(slots):
            for slot, c in zip(range(n_src - 1, 0, -1), gather(phase, zpk)):
                if slot in slots:
                    c.wait_recv()

            for slot in slots:
                rows = slice(own * slot, own * slot + own)
                u = unpack(field[phase, slot])
                y = u * xsrc[rows, :]
                y = y + pltpu.roll(y, 64, 1)
                y = y + pltpu.roll(y, 32, 1)
                high, low = split(jnp.where(l64 < 96, u, y))
                for at in (own * slot, J + own * slot):
                    rhs[at : at + own, 0:128] = high
                    rhs[at : at + own, 128:256] = low

        fields_of(range(4))
        fields_of(range(4, n_src))

        def multiply(pair, place):
            raw[place][...] = jnp.dot(mats[pair], rhs[...], preferred_element_type=F32)

        def combine(pair, place):
            for half in range(2):
                slot = 2 * pair + half
                base = half * 4 * own
                tail = rows_of(raw[place], slot, base, 3)
                for g in range(3):
                    mine[phase, slot, 16 * g : 16 * g + 16, :] = jnp.where(
                        lane < 96, rows_of(raw[place], slot, base, g), pltpu.roll(tail, 96 - 32 * g, 1)
                    )

        def exchange(pair):
            if pair in (1, 3):
                to_sibling(phase, pair // 2).start()
            if pair >= 4:
                if pair % 2 == 0:
                    to_sibling(phase, (pair - 4) // 2).wait_recv()
                for chip in (2 * pair - 8, 2 * pair - 7):
                    mine[phase, n_pair + chip] = mine[phase, n_pair + chip] + other[phase, chip]
                    if chip < n_pair - 1:
                        to_owner(phase, chip).start()

        first = phase == 1
        if first:
            other_tiles(0)
        for pair in range(n_pair):
            multiply(pair, pair % 2)
            if first and pair + 1 < n_pair:
                other_tiles(pair + 1)
            if pair:
                combine(pair - 1, (pair - 1) % 2)
                exchange(pair - 1)
        combine(n_pair - 1, 1)
        exchange(n_pair - 1)

        for chip in range(n_pair - 1):
            to_owner(phase, chip).wait_recv()

        total = mine[phase, n_tgt - 1]
        for chip in range(n_pair - 1):
            total = total + into[phase, chip]
        totals[...] = total

        if phase == 1:
            linear = (total - center * zpk[...]) / spread
            lpk[...] = linear
            field[2, 0] = linear
            for c in gather(2, lpk):
                c.start()

        def store_image(a, value):
            img_ref[phase - 1, a] = value

        emit(total, store_image)

        for q in range(2):
            to_sibling(phase, q).wait_send()
        for chip in range(n_pair - 1):
            to_owner(phase, chip).wait_send()

        return carry

    startup()
    one_phase(1, 0)
    one_phase(2, 0)
    noise = zpk[...]
    linear = lpk[...]
    quadratic = 2.0 * (totals[...] - center * linear) / spread - noise

    def store_disp(a, value):
        disp_ref[a] = value

    emit(0.5 * weights[0] * noise + weights[1] * linear + weights[2] * quadratic, store_disp)
    for c in gather(1, zpk) + gather(2, lpk):
        c.wait_send()


def body(positions, noise_vectors, spectrum_bounds):
    vmem = pl.BlockSpec(memory_space=pltpu.VMEM)
    dma = pltpu.SemaphoreType.DMA
    return pl.pallas_call(
        body_kernel,
        out_shape=(
            jax.ShapeDtypeStruct((3, 32, own), F32),
            jax.ShapeDtypeStruct((2, 3, 32, own), F32),
        ),
        in_specs=[pl.BlockSpec(memory_space=pltpu.HBM)] * 3,
        out_specs=(vmem, vmem),
        scratch_shapes=[
            pltpu.VMEM((3, own), F32),
            pltpu.VMEM((3, 32, own), F32),
            pltpu.SMEM((2,), F32),
            dma((3,)),
            pltpu.VMEM((128, 128), F32),
            pltpu.VMEM((8, 128), F32),
            pltpu.VMEM((n_tgt, 8, 128), F32),
            pltpu.VMEM((n_src, 8, 128), F32),
            pltpu.VMEM((8, J), F32),
            pltpu.VMEM((3, n_tgt * own, 128), F32),
            pltpu.VMEM((J, 128), F32),
            pltpu.VMEM((n_tgt * own, 128), F32),
            pltpu.VMEM((n_tgt // 2, 8 * own, 2 * J), BF16),
            pltpu.VMEM((8 * own, 256), F32),
            pltpu.VMEM((8 * own, 256), F32),
            pltpu.VMEM((packed, 128), F32),
            pltpu.VMEM((packed, 128), F32),
            pltpu.VMEM((3, n_src, packed, 128), F32),
            pltpu.VMEM((2 * J, 256), BF16),
            pltpu.VMEM((3, n_tgt, packed, 128), F32),
            pltpu.VMEM((3, n_pair, packed, 128), F32),
            pltpu.VMEM((3, n_pair, packed, 128), F32),
            pltpu.VMEM((packed, 128), F32),
            dma((n_tgt,)), dma((n_tgt,)), dma((n_src,)), dma((n_src,)),
            dma((3, n_src)), dma((3, n_src)), dma((3, 2)), dma((3, 2)),
            dma((3, n_pair)), dma((3, n_pair)),
        ],
        compiler_params=pltpu.CompilerParams(
            collective_id=0, has_side_effects=True, vmem_limit_bytes=64 << 20
        ),
        name="mobility_root",
    )(positions, noise_vectors, spectrum_bounds)


def solution(mesh):
    return jax.shard_map(
        body,
        mesh=mesh,
        in_specs=(P(None, ("blk", "tile")), P(None, None, ("blk", "tile")), P()),
        out_specs=(P(None, None, ("blk", "tile")), P(None, None, None, ("blk", "tile"))),
        check_vma=False,
    )
```

```python
import math

import jax
import jax.numpy as jnp
from jax import lax
from jax.experimental import pallas as pl
from jax.experimental.pallas import tpu as pltpu
from jax.sharding import PartitionSpec as P

MESH = pl.DeviceIdType.MESH
F32 = jnp.float32
BF16 = jnp.bfloat16

soft_core = 1e-06
node_count = 32
edge = (41.9 * 8192) ** (1.0 / 3.0)
middle = 0.5 * edge

own = 64
packed = 48
n_src = 8
n_tgt = 16
n_pair = n_tgt // 2
J = n_src * own

SOURCES = [(0, 0), (1, 0), (3, 0), (0, 1), (2, 0), (1, 1), (3, 1), (2, 1)]


def coords():
    block = lax.axis_index("blk")
    half = lax.axis_index("tile")
    return block // 16, (block // 8) % 2, (block // 2) % 4, block % 2, half


def source_peer(slot):
    dy, flip = SOURCES[slot]
    y, low, z, core, high = coords()
    return ((((y + dy) % 4) * 2 + (low + flip) % 2) * 4 + z) * 2 + core, high


TARGETS = [(2, 1), (2, 0), (1, 1), (3, 1), (1, 0), (3, 0), (0, 1), (0, 0)]
BACK = [0, 1, 3, 2, 5, 4, 6, 7]


def target_peer(slot):
    dz, flip = TARGETS[slot % n_pair]
    swap = 1 - slot // n_pair
    y, low, z, core, high = coords()
    return (
        ((y * 2 + (low + flip) % 2) * 4 + (z + dz) % 4) * 2 + (core + swap) % 2,
        (high + flip) % 2,
    )


def remote(src, dst, send, recv, device):
    return pltpu.make_async_remote_copy(
        src_ref=src, dst_ref=dst, send_sem=send, recv_sem=recv, device_id=device, device_id_type=MESH
    )


def lanes(rows):
    return lax.broadcasted_iota(jnp.int32, (rows, 128), 1)


def pack(full):
    tail = full[packed:own]
    moved = jnp.concatenate([pltpu.roll(tail, 96 - 32 * g, 1) if g < 3 else tail for g in range(3)], axis=0)
    return jnp.where(lanes(packed) < 96, full[:packed], moved)


def unpack(block):
    l16 = lanes(16)
    parts = [pltpu.roll(block[16 * g : 16 * g + 16], 32 + 32 * g, 1) for g in range(3)]
    tail = jnp.where(l16 < 32, parts[0], jnp.where(l16 < 64, parts[1], parts[2]))
    return jnp.concatenate([block, tail], axis=0)


def split(value):
    high = value.astype(BF16)
    low = (value - high.astype(F32)).astype(BF16)
    return high, low


def body_kernel(
    pos_hbm, noise_hbm, bounds_hbm, disp_ref, img_ref,
    pos_ref, noise_ref, bounds_ref, in_sem, square, ptile, tpos, spos, srow, bcol, xsrc, xtgt, mats, raw0, raw1,
    zpk, lpk, field, rhs, mine, other, into, totals,
    tp_send, tp_recv, sp_send, sp_recv, ag_send, ag_recv, sb_send, sb_recv, rs_send, rs_recv,
):
    loads = [
        pltpu.make_async_copy(src, dst, in_sem.at[k])
        for k, (src, dst) in enumerate(((pos_hbm, pos_ref), (noise_hbm, noise_ref), (bounds_hbm, bounds_ref)))
    ]
    for c in loads:
        c.start()
    barrier = pltpu.get_barrier_semaphore()
    for slot in range(n_tgt - 1):
        pl.semaphore_signal(barrier, inc=1, device_id=target_peer(slot), device_id_type=MESH)
    for slot in range(1, n_src):
        pl.semaphore_signal(barrier, inc=1, device_id=source_peer(slot), device_id_type=MESH)

    ptile[...] = jnp.zeros_like(ptile)
    square[...] = jnp.zeros_like(square)
    for c in loads:
        c.wait()
    ptile[0:3, 0:own] = pos_ref[...] - middle
    tile = ptile[...]
    tile = tile + pltpu.roll(tile, 64, 1)
    ptile[...] = tile
    tpos[n_tgt - 1] = tile
    spos[0] = tile
    for a in range(3):
        square[32 * a : 32 * a + 32, 0:own] = noise_ref[a]
    noise = pack(square[...].T[:own])
    zpk[...] = noise
    field[1, 0] = noise

    raw = (raw0, raw1)
    l64 = lanes(own)

    lane = lanes(16)

    def rows_of(source, slot, base, g):
        x = xtgt[pl.ds(pl.multiple_of(slot * own + 16 * g, 16), 16), :]
        r = []
        for m in range(4):
            rows = slice(base + own * m + 16 * g, base + own * m + 16 * g + 16)
            r.append(source[rows, 0:128] + source[rows, 128:256])
        e = [r[m] * x for m in (1, 2, 3)]
        e = [v + pltpu.roll(v, 64, 1) for v in e]
        here = jnp.where(lane < 32, e[0], jnp.where(lane < 64, e[1], e[2]))
        there = jnp.where(lane < 64, e[0], jnp.where(lane < 96, e[1], e[2]))
        return 0.5 * r[0] + here + pltpu.roll(there, 96, 1)

    def emit(value, store):
        square[0:own, :] = unpack(value)
        turned = square[...].T
        for a in range(3):
            store(a, turned[32 * a : 32 * a + 32, 0:own])

    def gather(phase, block):
        return [
            remote(block, field.at[phase, slot], ag_send.at[phase, slot], ag_recv.at[phase, slot], source_peer(slot))
            for slot in range(n_src - 1, 0, -1)
        ]

    pl.semaphore_wait(barrier, n_tgt - 1 + n_src - 1)
    spread_pos, target_pos = {}, {}
    for slot in range(n_src - 1, 0, -1):
        c = remote(ptile, spos.at[slot], sp_send.at[slot], sp_recv.at[slot], source_peer(slot))
        c.start()
        spread_pos[slot] = c
    for slot in range(n_tgt - 1):
        there = slot // n_pair * n_pair + BACK[slot % n_pair]
        c = remote(ptile, tpos.at[there], tp_send.at[slot], tp_recv.at[there], target_peer(slot))
        c.start()
        target_pos[there] = c

    for c in gather(1, zpk):
        c.start()

    lowest = bounds_ref[0]
    highest = bounds_ref[1]
    center = 0.5 * (highest + lowest)
    spread = 0.5 * (highest - lowest)
    q = lanes(8)
    angle = math.pi * (q.astype(F32) + 0.5) / node_count
    cosine = jnp.cos(angle)
    samples = jnp.where(q < node_count, jnp.sqrt(jnp.maximum(center + spread * cosine, 0.0)), 0.0)
    weights = [
        2.0 / node_count * jnp.sum(samples * factor, axis=1, keepdims=True)[0:1]
        for factor in (jnp.ones_like(cosine), cosine, jnp.cos(2.0 * angle))
    ]

    def pattern(c0, c1, c2, last):
        lane = lanes(c0.shape[0])
        return jnp.where(lane < 32, c0, jnp.where(lane < 64, c1, jnp.where(lane < 96, c2, last)))

    def fill(pair, row, count, p):
        rows = pl.ds(pair * 2 * own + row, count)
        c = [bcol[b, rows, :] for b in range(3)]
        cols = slice(128 * p, 128 * p + 128)
        o = [c[b] - srow[b : b + 1, cols] for b in range(3)]
        squared = o[0] * o[0] + o[1] * o[1] + o[2] * o[2] + soft_core
        inverse = lax.rsqrt(squared)
        inverse2 = inverse * inverse
        near = squared < 4.0
        scalar = jnp.where(near, 2.0 - 0.5625 * (squared * inverse), inverse * (1.5 + inverse2))
        dyadic = inverse * jnp.where(near, 0.0625, inverse2 * (0.5 - inverse2))
        for m, value in enumerate((scalar, dyadic * o[0], dyadic * o[1], dyadic * o[2])):
            high, low = split(value)
            at = (row // own * 4 + m) * own + row % own
            mats[pair, at : at + count, cols] = high
            mats[pair, at : at + count, J + 128 * p : J + 128 * p + 128] = low

    def near_tiles(step, carry):
        for row in range(0, 2 * own, 64):
            for p in (0, 1):
                fill(step // 2 * 4 + 2 + step % 2, row, 64, p)
        return carry

    def other_tiles(pair):
        for row in range(0, 2 * own, 64):
            for p in (range(4) if pair % 4 < 2 else (2, 3)):
                fill(pair, row, 64, p)

    def startup():
        first_half = lanes(8) < own

        def columns(tile):
            turned = tile.T
            return [jnp.broadcast_to(turned[:, b : b + 1], (128, 128)) for b in range(3)]

        def take_source(p):
            for slot in (2 * p, 2 * p + 1):
                if slot:
                    spread_pos[slot].wait_recv()
            tile = jnp.where(first_half, spos[2 * p], spos[2 * p + 1])
            srow[:, 128 * p : 128 * p + 128] = tile
            xsrc[128 * p : 128 * p + 128, :] = pattern(*columns(tile), 0.0)

        def take_target(p):
            for slot in (2 * p, 2 * p + 1):
                if slot < n_tgt - 1:
                    target_pos[slot].wait_recv()
            c = columns(jnp.where(first_half, tpos[2 * p], tpos[2 * p + 1]))
            for b in range(3):
                bcol[b, 128 * p : 128 * p + 128, :] = c[b]
            xtgt[128 * p : 128 * p + 128, :] = 1.5 * pattern(*c, -1.0)

        for p in (0, 1):
            take_source(p)
        for p in (7, 3, 6, 2):
            take_target(p)
        lax.fori_loop(0, 4, near_tiles, 0)
        for p in (2, 3):
            take_source(p)
        for p in (5, 4, 1, 0):
            take_target(p)

        for c in list(spread_pos.values()) + list(target_pos.values()):
            c.wait_send()

    def to_sibling(phase, quarter):
        some = pl.ds(quarter * 4, 4)
        return remote(
            mine.at[phase, some], other.at[phase, some], sb_send.at[phase, quarter], sb_recv.at[phase, quarter],
            target_peer(n_pair - 1),
        )

    def to_owner(phase, chip):
        return remote(
            mine.at[phase, n_pair + chip], into.at[phase, chip], rs_send.at[phase, chip], rs_recv.at[phase, chip],
            target_peer(n_pair + chip),
        )

    def one_phase(phase, carry):
        def fields_of(slots):
            for slot, c in zip(range(n_src - 1, 0, -1), gather(phase, zpk)):
                if slot in slots:
                    c.wait_recv()

            for slot in slots:
                rows = slice(own * slot, own * slot + own)
                u = unpack(field[phase, slot])
                y = u * xsrc[rows, :]
                y = y + pltpu.roll(y, 64, 1)
                y = y + pltpu.roll(y, 32, 1)
                high, low = split(jnp.where(l64 < 96, u, y))
                for at in (own * slot, J + own * slot):
                    rhs[at : at + own, 0:128] = high
                    rhs[at : at + own, 128:256] = low

        fields_of(range(n_src))

        def multiply(pair, place):
            raw[place][...] = jnp.dot(mats[pair], rhs[...], preferred_element_type=F32)

        def combine(pair, place):
            for half in range(2):
                slot = 2 * pair + half
                base = half * 4 * own
                tail = rows_of(raw[place], slot, base, 3)
                for g in range(3):
                    mine[phase, slot, 16 * g : 16 * g + 16, :] = jnp.where(
                        lane < 96, rows_of(raw[place], slot, base, g), pltpu.roll(tail, 96 - 32 * g, 1)
                    )

        def exchange(pair):
            if pair in (1, 3):
                to_sibling(phase, pair // 2).start()
            if pair in (5, 7):
                part = (pair - 5) // 2
                to_sibling(phase, part).wait_recv()
                for chip in range(4 * part, 4 * part + 4):
                    mine[phase, n_pair + chip] = mine[phase, n_pair + chip] + other[phase, chip]
                    if chip < n_pair - 1:
                        to_owner(phase, chip).start()

        first = phase == 1
        if first:
            other_tiles(0)
        for pair in range(n_pair):
            multiply(pair, pair % 2)
            if first and pair + 1 < n_pair:
                other_tiles(pair + 1)
            if pair:
                combine(pair - 1, (pair - 1) % 2)
                exchange(pair - 1)
        combine(n_pair - 1, 1)
        exchange(n_pair - 1)


        total = mine[phase, n_tgt - 1]
        for chip in range(n_pair - 1):
            to_owner(phase, chip).wait_recv()
            total = total + into[phase, chip]
        totals[...] = total

        if phase == 1:
            linear = (total - center * zpk[...]) / spread
            lpk[...] = linear
            field[2, 0] = linear
            for c in gather(2, lpk):
                c.start()

        if phase == 1:

            def store_image(a, value):
                img_ref[0, a] = value

            emit(total, store_image)

        for q in range(2):
            to_sibling(phase, q).wait_send()
        for chip in range(n_pair - 1):
            to_owner(phase, chip).wait_send()

        return carry

    startup()
    one_phase(1, 0)
    one_phase(2, 0)
    noise = zpk[...]
    linear = lpk[...]
    quadratic = 2.0 * (totals[...] - center * linear) / spread - noise

    square[0:own, :] = unpack(totals[...])
    square[own:, :] = unpack(0.5 * weights[0] * noise + weights[1] * linear + weights[2] * quadratic)
    turned = square[...].T
    moved = pltpu.roll(turned, 64, 1)
    for a in range(3):
        img_ref[1, a] = turned[32 * a : 32 * a + 32, 0:own]
        disp_ref[a] = moved[32 * a : 32 * a + 32, 0:own]
    for c in gather(1, zpk) + gather(2, lpk):
        c.wait_send()


def body(positions, noise_vectors, spectrum_bounds):
    vmem = pl.BlockSpec(memory_space=pltpu.VMEM)
    dma = pltpu.SemaphoreType.DMA
    return pl.pallas_call(
        body_kernel,
        out_shape=(
            jax.ShapeDtypeStruct((3, 32, own), F32),
            jax.ShapeDtypeStruct((2, 3, 32, own), F32),
        ),
        in_specs=[pl.BlockSpec(memory_space=pltpu.HBM)] * 3,
        out_specs=(vmem, vmem),
        scratch_shapes=[
            pltpu.VMEM((3, own), F32),
            pltpu.VMEM((3, 32, own), F32),
            pltpu.SMEM((2,), F32),
            dma((3,)),
            pltpu.VMEM((128, 128), F32),
            pltpu.VMEM((8, 128), F32),
            pltpu.VMEM((n_tgt, 8, 128), F32),
            pltpu.VMEM((n_src, 8, 128), F32),
            pltpu.VMEM((8, J), F32),
            pltpu.VMEM((3, n_tgt * own, 128), F32),
            pltpu.VMEM((J, 128), F32),
            pltpu.VMEM((n_tgt * own, 128), F32),
            pltpu.VMEM((n_tgt // 2, 8 * own, 2 * J), BF16),
            pltpu.VMEM((8 * own, 256), F32),
            pltpu.VMEM((8 * own, 256), F32),
            pltpu.VMEM((packed, 128), F32),
            pltpu.VMEM((packed, 128), F32),
            pltpu.VMEM((3, n_src, packed, 128), F32),
            pltpu.VMEM((2 * J, 256), BF16),
            pltpu.VMEM((3, n_tgt, packed, 128), F32),
            pltpu.VMEM((3, n_pair, packed, 128), F32),
            pltpu.VMEM((3, n_pair, packed, 128), F32),
            pltpu.VMEM((packed, 128), F32),
            dma((n_tgt,)), dma((n_tgt,)), dma((n_src,)), dma((n_src,)),
            dma((3, n_src)), dma((3, n_src)), dma((3, 2)), dma((3, 2)),
            dma((3, n_pair)), dma((3, n_pair)),
        ],
        compiler_params=pltpu.CompilerParams(
            collective_id=0, has_side_effects=True, vmem_limit_bytes=64 << 20
        ),
        name="mobility_root",
    )(positions, noise_vectors, spectrum_bounds)


def solution(mesh):
    return jax.shard_map(
        body,
        mesh=mesh,
        in_specs=(P(None, ("blk", "tile")), P(None, None, ("blk", "tile")), P()),
        out_specs=(P(None, None, ("blk", "tile")), P(None, None, None, ("blk", "tile"))),
        check_vma=False,
    )
```

```python
import math

import jax
import jax.numpy as jnp
from jax import lax
from jax.experimental import pallas as pl
from jax.experimental.pallas import tpu as pltpu
from jax.sharding import PartitionSpec as P

MESH = pl.DeviceIdType.MESH
F32 = jnp.float32
BF16 = jnp.bfloat16

soft_core = 1e-06
node_count = 32
edge = (41.9 * 8192) ** (1.0 / 3.0)
middle = 0.5 * edge

own = 64
packed = 48
n_src = 8
n_tgt = 16
n_pair = n_tgt // 2
J = n_src * own

SOURCES = [(0, 0), (1, 0), (3, 0), (0, 1), (2, 0), (1, 1), (3, 1), (2, 1)]


def coords():
    block = lax.axis_index("blk")
    half = lax.axis_index("tile")
    return block // 16, (block // 8) % 2, (block // 2) % 4, block % 2, half


def source_peer(slot):
    dy, flip = SOURCES[slot]
    y, low, z, core, high = coords()
    return ((((y + dy) % 4) * 2 + (low + flip) % 2) * 4 + z) * 2 + core, high


TARGETS = [(2, 1), (2, 0), (1, 1), (3, 1), (1, 0), (3, 0), (0, 1), (0, 0)]
BACK = [0, 1, 3, 2, 5, 4, 6, 7]


def target_peer(slot):
    dz, flip = TARGETS[slot % n_pair]
    swap = 1 - slot // n_pair
    y, low, z, core, high = coords()
    return (
        ((y * 2 + (low + flip) % 2) * 4 + (z + dz) % 4) * 2 + (core + swap) % 2,
        (high + flip) % 2,
    )


def remote(src, dst, send, recv, device):
    return pltpu.make_async_remote_copy(
        src_ref=src, dst_ref=dst, send_sem=send, recv_sem=recv, device_id=device, device_id_type=MESH
    )


def lanes(rows):
    return lax.broadcasted_iota(jnp.int32, (rows, 128), 1)


def pack(full):
    tail = full[packed:own]
    moved = jnp.concatenate([pltpu.roll(tail, 96 - 32 * g, 1) if g < 3 else tail for g in range(3)], axis=0)
    return jnp.where(lanes(packed) < 96, full[:packed], moved)


def unpack(block):
    l16 = lanes(16)
    parts = [pltpu.roll(block[16 * g : 16 * g + 16], 32 + 32 * g, 1) for g in range(3)]
    tail = jnp.where(l16 < 32, parts[0], jnp.where(l16 < 64, parts[1], parts[2]))
    return jnp.concatenate([block, tail], axis=0)


def split(value):
    high = value.astype(BF16)
    low = (value - high.astype(F32)).astype(BF16)
    return high, low


def body_kernel(
    pos_hbm, noise_hbm, bounds_hbm, disp_ref, img_ref,
    pos_ref, noise_ref, bounds_ref, in_sem, square, ptile, tpos, spos, srow, bcol, xsrc, xtgt, mats, raw0, raw1,
    zpk, lpk, field, rhs, mine, other, into, totals,
    tp_send, tp_recv, sp_send, sp_recv, ag_send, ag_recv, sb_send, sb_recv, rs_send, rs_recv,
):
    loads = [
        pltpu.make_async_copy(src, dst, in_sem.at[k])
        for k, (src, dst) in enumerate(((pos_hbm, pos_ref), (noise_hbm, noise_ref), (bounds_hbm, bounds_ref)))
    ]
    for c in loads:
        c.start()
    barrier = pltpu.get_barrier_semaphore()
    for slot in range(n_tgt - 1):
        pl.semaphore_signal(barrier, inc=1, device_id=target_peer(slot), device_id_type=MESH)
    for slot in range(1, n_src):
        pl.semaphore_signal(barrier, inc=1, device_id=source_peer(slot), device_id_type=MESH)

    ptile[...] = jnp.zeros_like(ptile)
    square[...] = jnp.zeros_like(square)
    for c in loads:
        c.wait()
    ptile[0:3, 0:own] = pos_ref[...] - middle
    tile = ptile[...]
    tile = tile + pltpu.roll(tile, 64, 1)
    ptile[...] = tile
    tpos[n_tgt - 1] = tile
    spos[0] = tile
    for a in range(3):
        square[32 * a : 32 * a + 32, 0:own] = noise_ref[a]
    noise = pack(square[...].T[:own])
    zpk[...] = noise
    field[1, 0] = noise

    raw = (raw0, raw1)
    l64 = lanes(own)

    lane = lanes(16)

    def rows_of(source, slot, base, g):
        x = xtgt[pl.ds(pl.multiple_of(slot * own + 16 * g, 16), 16), :]
        r = []
        for m in range(4):
            rows = slice(base + own * m + 16 * g, base + own * m + 16 * g + 16)
            r.append(source[rows, 0:128] + source[rows, 128:256])
        e = [r[m] * x for m in (1, 2, 3)]
        e = [v + pltpu.roll(v, 64, 1) for v in e]
        here = jnp.where(lane < 32, e[0], jnp.where(lane < 64, e[1], e[2]))
        there = jnp.where(lane < 64, e[0], jnp.where(lane < 96, e[1], e[2]))
        return 0.5 * r[0] + here + pltpu.roll(there, 96, 1)

    def emit(value, store):
        square[0:own, :] = unpack(value)
        turned = square[...].T
        for a in range(3):
            store(a, turned[32 * a : 32 * a + 32, 0:own])

    def gather(phase, block):
        return [
            remote(block, field.at[phase, slot], ag_send.at[phase, slot], ag_recv.at[phase, slot], source_peer(slot))
            for slot in range(n_src - 1, 0, -1)
        ]

    pl.semaphore_wait(barrier, n_tgt - 1 + n_src - 1)
    spread_pos, target_pos = {}, {}
    for slot in range(n_src - 1, 0, -1):
        c = remote(ptile, spos.at[slot], sp_send.at[slot], sp_recv.at[slot], source_peer(slot))
        c.start()
        spread_pos[slot] = c
    for slot in range(n_tgt - 1):
        there = slot // n_pair * n_pair + BACK[slot % n_pair]
        c = remote(ptile, tpos.at[there], tp_send.at[slot], tp_recv.at[there], target_peer(slot))
        c.start()
        target_pos[there] = c

    for c in gather(1, zpk):
        c.start()

    lowest = bounds_ref[0]
    highest = bounds_ref[1]
    center = 0.5 * (highest + lowest)
    spread = 0.5 * (highest - lowest)
    q = lanes(8)
    angle = math.pi * (q.astype(F32) + 0.5) / node_count
    cosine = jnp.cos(angle)
    samples = jnp.where(q < node_count, jnp.sqrt(jnp.maximum(center + spread * cosine, 0.0)), 0.0)
    weights = [
        2.0 / node_count * jnp.sum(samples * factor, axis=1, keepdims=True)[0:1]
        for factor in (jnp.ones_like(cosine), cosine, jnp.cos(2.0 * angle))
    ]

    def pattern(c0, c1, c2, last):
        lane = lanes(c0.shape[0])
        return jnp.where(lane < 32, c0, jnp.where(lane < 64, c1, jnp.where(lane < 96, c2, last)))

    def fill(pair, row, count, p):
        rows = pl.ds(pair * 2 * own + row, count)
        c = [bcol[b, rows, :] for b in range(3)]
        cols = slice(128 * p, 128 * p + 128)
        o = [c[b] - srow[b : b + 1, cols] for b in range(3)]
        squared = o[0] * o[0] + o[1] * o[1] + o[2] * o[2] + soft_core
        inverse = lax.rsqrt(squared)
        inverse2 = inverse * inverse
        near = squared < 4.0
        scalar = jnp.where(near, 2.0 - 0.5625 * (squared * inverse), inverse * (1.5 + inverse2))
        dyadic = inverse * jnp.where(near, 0.0625, inverse2 * (0.5 - inverse2))
        for m, value in enumerate((scalar, dyadic * o[0], dyadic * o[1], dyadic * o[2])):
            high, low = split(value)
            at = (row // own * 4 + m) * own + row % own
            mats[pair, at : at + count, cols] = high
            mats[pair, at : at + count, J + 128 * p : J + 128 * p + 128] = low

    def near_tiles(step, carry):
        for row in range(0, 2 * own, 64):
            for p in (0, 1):
                fill(step // 2 * 4 + 2 + step % 2, row, 64, p)
        return carry

    def other_tiles(pair):
        for row in range(0, 2 * own, 64):
            for p in (range(4) if pair % 4 < 2 else (2, 3)):
                fill(pair, row, 64, p)

    def startup():
        first_half = lanes(8) < own

        def columns(tile):
            turned = tile.T
            return [jnp.broadcast_to(turned[:, b : b + 1], (128, 128)) for b in range(3)]

        def take_source(p):
            for slot in (2 * p, 2 * p + 1):
                if slot:
                    spread_pos[slot].wait_recv()
            tile = jnp.where(first_half, spos[2 * p], spos[2 * p + 1])
            srow[:, 128 * p : 128 * p + 128] = tile
            xsrc[128 * p : 128 * p + 128, :] = pattern(*columns(tile), 0.0)

        def take_target(p):
            for slot in (2 * p, 2 * p + 1):
                if slot < n_tgt - 1:
                    target_pos[slot].wait_recv()
            c = columns(jnp.where(first_half, tpos[2 * p], tpos[2 * p + 1]))
            for b in range(3):
                bcol[b, 128 * p : 128 * p + 128, :] = c[b]
            xtgt[128 * p : 128 * p + 128, :] = 1.5 * pattern(*c, -1.0)

        for p in (0, 1):
            take_source(p)
        for p in (7, 3, 6, 2):
            take_target(p)
        lax.fori_loop(0, 4, near_tiles, 0)
        for p in (2, 3):
            take_source(p)
        for p in (5, 4, 1, 0):
            take_target(p)

        for c in list(spread_pos.values()) + list(target_pos.values()):
            c.wait_send()

    def to_sibling(phase, quarter):
        some = pl.ds(quarter * 4, 4)
        return remote(
            mine.at[phase, some], other.at[phase, some], sb_send.at[phase, quarter], sb_recv.at[phase, quarter],
            target_peer(n_pair - 1),
        )

    def to_owner(phase, chip):
        return remote(
            mine.at[phase, n_pair + chip], into.at[phase, chip], rs_send.at[phase, chip], rs_recv.at[phase, chip],
            target_peer(n_pair + chip),
        )

    def one_phase(phase, carry):
        def fields_of(slots):
            for slot, c in zip(range(n_src - 1, 0, -1), gather(phase, zpk)):
                if slot in slots:
                    c.wait_recv()

            for slot in slots:
                rows = slice(own * slot, own * slot + own)
                u = unpack(field[phase, slot])
                y = u * xsrc[rows, :]
                y = y + pltpu.roll(y, 64, 1)
                y = y + pltpu.roll(y, 32, 1)
                high, low = split(jnp.where(l64 < 96, u, y))
                for at in (own * slot, J + own * slot):
                    rhs[at : at + own, 0:128] = high
                    rhs[at : at + own, 128:256] = low

        fields_of(range(n_src))

        def multiply(pair, place):
            raw[place][...] = jnp.dot(mats[pair], rhs[...], preferred_element_type=F32)

        def combine(pair, place):
            for half in range(2):
                slot = 2 * pair + half
                base = half * 4 * own
                tail = rows_of(raw[place], slot, base, 3)
                for g in range(3):
                    mine[phase, slot, 16 * g : 16 * g + 16, :] = jnp.where(
                        lane < 96, rows_of(raw[place], slot, base, g), pltpu.roll(tail, 96 - 32 * g, 1)
                    )

        def exchange(pair):
            if pair in (1, 3):
                to_sibling(phase, pair // 2).start()
            if pair in (5, 7):
                part = (pair - 5) // 2
                to_sibling(phase, part).wait_recv()
                for chip in range(4 * part, 4 * part + 4):
                    mine[phase, n_pair + chip] = mine[phase, n_pair + chip] + other[phase, chip]
                    if chip < n_pair - 1:
                        to_owner(phase, chip).start()

        first = phase == 1
        if first:
            other_tiles(0)
        for pair in range(n_pair):
            multiply(pair, pair % 2)
            if first and pair + 1 < n_pair:
                other_tiles(pair + 1)
            if pair:
                combine(pair - 1, (pair - 1) % 2)
                exchange(pair - 1)
        combine(n_pair - 1, 1)
        exchange(n_pair - 1)


        total = mine[phase, n_tgt - 1]
        for chip in range(n_pair - 1):
            to_owner(phase, chip).wait_recv()
            total = total + into[phase, chip]
        totals[...] = total

        if phase == 1:
            linear = (total - center * zpk[...]) / spread
            lpk[...] = linear
            field[2, 0] = linear
            for c in gather(2, lpk):
                c.start()

        if phase == 1:

            def store_image(a, value):
                img_ref[0, a] = value

            emit(total, store_image)
            field[0, 0] = (0.5 * weights[0] - weights[2]) * zpk[...] + (
                weights[1] - 2.0 * center / spread * weights[2]
            ) * linear

        for q in range(2):
            to_sibling(phase, q).wait_send()
        for chip in range(n_pair - 1):
            to_owner(phase, chip).wait_send()

        return carry

    startup()
    one_phase(1, 0)
    one_phase(2, 0)
    square[0:own, :] = unpack(totals[...])
    square[own:, :] = unpack(field[0, 0] + 2.0 / spread * weights[2] * totals[...])
    turned = square[...].T
    moved = pltpu.roll(turned, 64, 1)
    for a in range(3):
        img_ref[1, a] = turned[32 * a : 32 * a + 32, 0:own]
        disp_ref[a] = moved[32 * a : 32 * a + 32, 0:own]
    for c in gather(1, zpk) + gather(2, lpk):
        c.wait_send()


def body(positions, noise_vectors, spectrum_bounds):
    vmem = pl.BlockSpec(memory_space=pltpu.VMEM)
    dma = pltpu.SemaphoreType.DMA
    return pl.pallas_call(
        body_kernel,
        out_shape=(
            jax.ShapeDtypeStruct((3, 32, own), F32),
            jax.ShapeDtypeStruct((2, 3, 32, own), F32),
        ),
        in_specs=[pl.BlockSpec(memory_space=pltpu.HBM)] * 3,
        out_specs=(vmem, vmem),
        scratch_shapes=[
            pltpu.VMEM((3, own), F32),
            pltpu.VMEM((3, 32, own), F32),
            pltpu.SMEM((2,), F32),
            dma((3,)),
            pltpu.VMEM((128, 128), F32),
            pltpu.VMEM((8, 128), F32),
            pltpu.VMEM((n_tgt, 8, 128), F32),
            pltpu.VMEM((n_src, 8, 128), F32),
            pltpu.VMEM((8, J), F32),
            pltpu.VMEM((3, n_tgt * own, 128), F32),
            pltpu.VMEM((J, 128), F32),
            pltpu.VMEM((n_tgt * own, 128), F32),
            pltpu.VMEM((n_tgt // 2, 8 * own, 2 * J), BF16),
            pltpu.VMEM((8 * own, 256), F32),
            pltpu.VMEM((8 * own, 256), F32),
            pltpu.VMEM((packed, 128), F32),
            pltpu.VMEM((packed, 128), F32),
            pltpu.VMEM((3, n_src, packed, 128), F32),
            pltpu.VMEM((2 * J, 256), BF16),
            pltpu.VMEM((3, n_tgt, packed, 128), F32),
            pltpu.VMEM((3, n_pair, packed, 128), F32),
            pltpu.VMEM((3, n_pair, packed, 128), F32),
            pltpu.VMEM((packed, 128), F32),
            dma((n_tgt,)), dma((n_tgt,)), dma((n_src,)), dma((n_src,)),
            dma((3, n_src)), dma((3, n_src)), dma((3, 2)), dma((3, 2)),
            dma((3, n_pair)), dma((3, n_pair)),
        ],
        compiler_params=pltpu.CompilerParams(
            collective_id=0, has_side_effects=True, vmem_limit_bytes=64 << 20
        ),
        name="mobility_root",
    )(positions, noise_vectors, spectrum_bounds)


def solution(mesh):
    return jax.shard_map(
        body,
        mesh=mesh,
        in_specs=(P(None, ("blk", "tile")), P(None, None, ("blk", "tile")), P()),
        out_specs=(P(None, None, ("blk", "tile")), P(None, None, None, ("blk", "tile"))),
        check_vma=False,
    )
```
